32 devices in a mesh: pop: 2 (over y), ctx: 4 (over z), exp: 2 (over x), tp: 2 (over core).
Axes of the slice: x: 2, y: 2, z: 4, core: 2. Of those that a mesh axis runs over, the one named last changes fastest.
Arguments:
- tokens: bfloat16 [2048, 2688], P(('pop', 'ctx', 'tp')), parts along dimension 0, may hold values from -6 to 6
- routes: int32 [2048, 6], P(('pop', 'ctx', 'tp')), parts along dimension 0, may hold values from 0 to 15, all different within a row; in each aligned block of 128 rows (0 to 127, 128 to 255, ...) at most 64 rows name the same one
- route_gates: float32 [2048, 6], P(('pop', 'ctx', 'tp')), parts along dimension 0, may hold values from 0.05 to 1
- up_weight: bfloat16 [16, 2688, 1536], P(('ctx', 'tp'), None, 'exp'), may hold values from -0.125 to 0.125
- down_weight: bfloat16 [16, 1536, 2688], P(('ctx', 'tp'), None, 'exp'), may hold values from -0.15625 to 0.15625
- factor_seeds: int32 [32, 4], P(('pop', 'ctx', 'tp')), parts along dimension 0, may hold values from 0 to 15
- up_left: bfloat16 [16, 2688], replicated, may hold values from -0.125 to 0.125
- up_right: bfloat16 [16, 1536], P(None, 'exp'), may hold values from -3 to 3
- down_left: bfloat16 [16, 1536], replicated, may hold values from -0.15625 to 0.15625
- down_right: bfloat16 [16, 2688], P(None, 'exp'), may hold values from -3 to 3
Outputs:
- moe_output: bfloat16 [2048, 2688], P(('pop', 'ctx', 'tp'), 'exp'), parts along dimension 0
The draws below stay inside these ranges and needn't reach their ends.
There are 2 independent parts, one for each index of `pop`. The reference program is written for one: setup_inputs(seed, part) draws one part's arguments, and reference() takes and returns one part's arrays. A program takes and returns all parts, laid end to end along the dimension named above; an argument that names none is the same for every part. Nothing has to cross between parts.
Inputs may be any that keep to these rules, and one draw needn't show every extreme that they name: `routes`: each row names 6 different experts. Among the 128 rows of one device (aligned blocks of 128 rows) no expert is named more than 64 times, and in every draw some expert is named exactly 64 times in some block.
All inputs are finite; a program needn't handle non-finite values.
Results may differ from the reference program's by a relative error of at most 0.0057.
Values may be sent and summed in bfloat16 or wider, within the bound.
A program may use at most 64 MiB of HBM per device.

```python
import math
import jax
import jax.numpy as jnp
import numpy as np
from jax import lax

D = 2688
TOP = 6
HID = 1536
NFAC = 16
TOK_DEV = 128
EXPERTS = 16
CAP = 64
TOKENS = 1024
N_CTX = 4
N_TP = 2


def place_ends(result, key, smallest, largest):
    extent = result.shape
    spot = [jax.random.randint(jax.random.fold_in(key, axis), (), 0, extent[axis]) for axis in range(len(extent))]
    result = result.at[tuple(spot)].set(smallest)
    longest = extent.index(max(extent))
    spot[longest] = (spot[longest] + 1) % extent[longest]
    return result.at[tuple(spot)].set(largest)


def steps_of(stream_key, shape, shards, low, top_value):
    gain = 1.0
    for dim, blocks in shards:
        heights = jax.random.uniform(jax.random.fold_in(jax.random.fold_in(stream_key, 6), dim), (blocks,), jnp.float32, low / len(shards), top_value / len(shards))
        gain = gain * jnp.repeat(jnp.exp(heights), shape[dim] // blocks).reshape((-1,) + (1,) * (len(shape) - 1 - dim))
    return gain


def shared_out(own_key, own, number, rows, number_of, top, limit, lean):
    sequence = jax.random.permutation(own_key, number_of)
    heavy_load, common = portions_of(number_of, rows * top, limit, lean, True), portions_of(number_of, rows * top, limit, lean, False)
    places = jnp.arange(number_of)

    def named(tallies, turn):
        used = int((tallies > 0).sum())
        fixed = max(1, used // 4)
        passed = fixed + (places - fixed + turn * (used - fixed)) % max(1, number_of - fixed)
        return jnp.zeros((number_of,), jnp.int32).at[sequence[jnp.where(places < fixed, places, passed)]].set(jnp.asarray(tallies, jnp.int32))

    tallies = jnp.where(number % 4 == 0, named(heavy_load, number // 4), named(common, number - number // 4 - 1))
    mixed = jax.random.permutation(jax.random.fold_in(own, 3), number_of)
    giver, sink = mixed[0:number_of // 2 * 2:2], mixed[1:number_of // 2 * 2:2]
    slack = jnp.minimum(tallies[giver] - 1, limit - tallies[sink]) // 2
    slack = jnp.where((giver == sequence[0]) | (sink == sequence[0]) | (tallies[sink] == 0), 0, jnp.maximum(slack, 0))
    passed = jax.random.randint(jax.random.fold_in(own, 4), (number_of // 2,), 0, 1 << 20) % (slack + 1)
    tallies = tallies.at[giver].add(-passed).at[sink].add(passed)
    labels = jnp.searchsorted(jnp.cumsum(tallies), jnp.arange(rows * top), side="right").astype(jnp.int32)
    table = labels.reshape(top, rows).T
    table = table[jax.random.permutation(jax.random.fold_in(own, 1), rows)]
    turn = jax.random.randint(jax.random.fold_in(own, 2), (rows, 1), 0, top)
    return jnp.take_along_axis(table, (jnp.arange(top)[None, :] + turn) % top, axis=1)


def portions_of(number_of, total, most, lean, full):
    loads = [(1 << 20) // math.isqrt(rank ** lean) + 1 for rank in range(1, number_of + 1)]
    largest = most if full else min(most, max(-(-total // number_of), total * loads[0] // sum(loads)))
    least = 1 if total - largest >= number_of - 1 else 0
    given, rest = [largest] + [least] * (number_of - 1), total - largest - least * (number_of - 1)
    while rest > 0:
        free = [i for i in range(1, number_of) if given[i] < largest] or [i for i in range(1, number_of) if given[i] < most]
        whole, left = sum([loads[i] for i in free]), rest
        for i in free:
            extra = min(most - given[i], max(1, left * loads[i] // whole), rest)
            given[i] = given[i] + extra
            rest = rest - extra
    return np.array(given)


def noise(stream_key, extent, width, most, cuts=(), kind=jnp.bfloat16):
    factor_of = steps_of(stream_key, extent, cuts, -0.22, 0.18) if cuts else 1.0
    array = jax.random.normal(stream_key, extent, jnp.float32) * width * factor_of
    return jnp.minimum(jnp.maximum(array, -most), most).astype(kind)


def setup_inputs(seed: int = 0, part: int = 0) -> dict:
    seeds = jax.random.split(jax.random.key(seed), 11)
    part_keys = jax.random.split(jax.random.fold_in(seeds[10], part), 11)
    tokens = noise(part_keys[0], (TOKENS, D), 1.0, 6.0, ((0, 8),))
    routes_keys = jax.random.split(jax.random.fold_in(part_keys[1], 1), TOKENS // TOK_DEV)
    routes_turns = jax.random.permutation(jax.random.fold_in(part_keys[1], 3), TOKENS // TOK_DEV)
    routes = jax.vmap(lambda own, number: shared_out(jax.random.fold_in(part_keys[1], 2), own, number, TOK_DEV, EXPERTS, TOP, CAP, 2))(routes_keys, routes_turns).reshape((TOKENS, TOP))
    route_gates = jnp.clip(jnp.exp(math.log(1.0) - 2.9957323 * jax.random.uniform(part_keys[2], (TOKENS, TOP), jnp.float32) ** steps_of(part_keys[2], (TOKENS, TOP), ((0, 8),), -0.2, 0.2)), 0.05, 1.0)
    up_weight = noise(seeds[3], (EXPERTS, D, HID), D ** -0.5, 0.125, ((0, 8), (2, 2)))
    down_weight = noise(seeds[4], (EXPERTS, HID, D), HID ** -0.5, 0.15625, ((0, 8), (2, 2)))
    factor_seeds = place_ends(jax.random.randint(part_keys[5], (EXPERTS, 4), 0, NFAC), jax.random.fold_in(part_keys[5], 1), 0, NFAC - 1).astype(jnp.int32)
    up_left = noise(seeds[6], (NFAC, D), D ** -0.5, 0.125)
    up_right = noise(seeds[7], (NFAC, HID), 0.5, 3.0, ((1, 2),))
    down_left = noise(seeds[8], (NFAC, HID), HID ** -0.5, 0.15625)
    down_right = noise(seeds[9], (NFAC, D), 0.5, 3.0, ((1, 2),))
    return dict(tokens=tokens, routes=routes, route_gates=route_gates, up_weight=up_weight, down_weight=down_weight, factor_seeds=factor_seeds, up_left=up_left, up_right=up_right, down_left=down_left, down_right=down_right)


def reference(tokens, routes, route_gates, up_weight, down_weight, factor_seeds, up_left, up_right, down_left, down_right):
    flat_routes = routes.reshape(-1)
    normed = route_gates / jnp.sum(route_gates, axis=1, keepdims=True)
    flat_gates = normed.reshape(-1)
    slot_limit = N_CTX * N_TP * CAP

    def expert_step(summed, expert_id):
        ordering = jnp.argsort((flat_routes != expert_id).astype(jnp.int32), stable=True)[:slot_limit]
        is_live = flat_routes[ordering] == expert_id
        token_ids = (ordering // TOP).astype(jnp.int32)
        token_rows = tokens[token_ids]
        chosen = factor_seeds[expert_id]
        up_act = jnp.dot(token_rows, up_weight[expert_id], preferred_element_type=jnp.float32)
        low_rank = jnp.dot(token_rows, up_left[chosen[0]], preferred_element_type=jnp.float32)
        up_act = up_act + low_rank[:, None] * up_right[chosen[1]].astype(jnp.float32)
        hidden = (jnp.maximum(up_act, 0.0) ** 2).astype(jnp.bfloat16)
        down_act = jnp.dot(hidden, down_weight[expert_id], preferred_element_type=jnp.float32)
        down_rank = jnp.dot(hidden, down_left[chosen[2]], preferred_element_type=jnp.float32)
        down_act = down_act + down_rank[:, None] * down_right[chosen[3]].astype(jnp.float32)
        rounded = lax.optimization_barrier(down_act.astype(jnp.bfloat16))
        output = rounded.astype(jnp.float32)
        weight = jnp.where(is_live, flat_gates[ordering], jnp.zeros((), flat_gates.dtype))
        summed = summed.at[token_ids].add(weight[:, None] * output)
        return summed, None

    summed, _ = lax.scan(expert_step, jnp.zeros((TOKENS, D), jnp.float32), jnp.arange(EXPERTS, dtype=jnp.int32))
    return summed.astype(jnp.bfloat16)
```

```python
import functools

import jax
import jax.numpy as jnp
from jax import lax
from jax.experimental import pallas as pl
from jax.experimental.pallas import tpu as pltpu
from jax.sharding import PartitionSpec as P


def pick_rows(factor_table, indices):
    chooser = (
        indices[:, None] == jnp.arange(factor_table.shape[0], dtype=jnp.int32)[None, :]
    ).astype(factor_table.dtype)
    return jnp.dot(chooser, factor_table, preferred_element_type=jnp.float32).astype(
        factor_table.dtype
    )


def general_path(
    tokens,
    routes,
    route_gates,
    up_weight,
    down_weight,
    factor_seeds,
    up_left,
    up_right,
    down_left,
    down_right,
):
    dest_count = lax.axis_size("ctx") * lax.axis_size("tp")
    local_experts = up_weight.shape[0]
    experts_all = dest_count * local_experts
    tok_count, top_count = routes.shape
    capacity = 4 * tok_count * top_count // (3 * experts_all)
    model_width = tokens.shape[1]
    flat_routes = routes.reshape(-1)
    chooser = (flat_routes[:, None] == jnp.arange(experts_all, dtype=jnp.int32)[None, :]).astype(
        jnp.int32
    )
    earlier = jnp.cumsum(chooser, axis=0) - chooser
    slot_index = jnp.sum(earlier * chooser, axis=1)
    target = flat_routes * capacity + slot_index
    pair_token = jnp.arange(tok_count * top_count, dtype=jnp.int32) // top_count + 1
    owner_token = jnp.zeros((experts_all * capacity,), jnp.int32).at[target].set(pair_token)
    source_row = jnp.where(owner_token > 0, owner_token - 1, tok_count)
    padded_tokens = jnp.concatenate([tokens, jnp.zeros((1, model_width), tokens.dtype)], axis=0)
    token_rows = padded_tokens[source_row]
    outgoing = token_rows.reshape(dest_count, local_experts, capacity, model_width)
    left_up = pick_rows(up_left, factor_seeds[:, 0])
    right_up = pick_rows(up_right, factor_seeds[:, 1])
    left_down = pick_rows(down_left, factor_seeds[:, 2])
    right_down = pick_rows(down_right, factor_seeds[:, 3])
    buffer = lax.all_to_all(outgoing, ("ctx", "tp"), split_axis=0, concat_axis=0, tiled=True)
    up_act = jnp.einsum("slcd,ldh->slch", buffer, up_weight, preferred_element_type=jnp.float32)
    low_rank = jnp.einsum("slcd,ld->slc", buffer, left_up, preferred_element_type=jnp.float32)
    up_act = up_act + low_rank[..., None] * right_up[None, :, None, :].astype(jnp.float32)
    hidden = (jnp.maximum(up_act, 0.0) ** 2).astype(jnp.bfloat16)
    full_hidden = lax.all_gather(hidden, "exp", axis=3, tiled=True)
    summed = jnp.einsum(
        "slch,lhd->slcd", full_hidden, down_weight, preferred_element_type=jnp.float32
    )
    rank_sum = jnp.einsum(
        "slch,lh->slc", full_hidden, left_down, preferred_element_type=jnp.float32
    )
    result = (
        summed + rank_sum[..., None] * right_down[None, :, None, :].astype(jnp.float32)
    ).astype(jnp.bfloat16)
    returned = lax.all_to_all(result, ("ctx", "tp"), split_axis=0, concat_axis=0, tiled=True)
    back_rows = returned.reshape(experts_all * capacity, -1)
    picked = back_rows[target]
    normed = (route_gates / jnp.sum(route_gates, axis=1, keepdims=True)).reshape(-1)
    weighted = picked.astype(jnp.float32) * normed[:, None]
    moe_output = jnp.sum(weighted.reshape(tok_count, top_count, -1), axis=1)
    return moe_output.astype(jnp.bfloat16)


def fused_kernel(
    cfg,
    meta_ref, tokens_ref, lu_ref, ru_ref, ld_ref, rd_ref, wu_hbm, wd_hbm,
    out_ref,
    rows, meta_in, wu, wd, xs, hid_own, hid_rem, scaled, own_part, pair_out, pair_in,
    far_out, far_in, kept,
    z_s, z_r, x_s, x_r, cz_s, cz_r, cx_s, cx_r, h_s, h_r, p_s, p_r, o_s, o_r, m_s, m_r, loc,
):
    ctx_n, tp_n, local_n, cap, zr = cfg
    tok = tokens_ref.shape[0]
    half = wu.shape[2]
    xr = tok - zr
    c, e, t = lax.axis_index("ctx"), lax.axis_index("exp"), lax.axis_index("tp")
    other_e, other_t = 1 - e, 1 - t
    me = c * tp_n + t
    n = ctx_n * tp_n
    bf, f32 = jnp.bfloat16, jnp.float32

    load_up = pltpu.make_async_copy(wu_hbm, wu, loc.at[0])
    load_down = pltpu.make_async_copy(wd_hbm, wd, loc.at[1])
    load_tok = pltpu.make_async_copy(tokens_ref, rows.at[c, t], loc.at[2])
    load_tok.start()
    load_up.start()
    load_down.start()

    barrier = pltpu.get_barrier_semaphore()
    for k in range(1, n):
        peer = (me + k) % n
        pl.semaphore_signal(
            barrier, inc=1, device_id={"ctx": peer // tp_n, "tp": peer % tp_n},
            device_id_type=pl.DeviceIdType.MESH,
        )
    pl.semaphore_signal(
        barrier, inc=1, device_id={"exp": other_e}, device_id_type=pl.DeviceIdType.MESH
    )
    pl.semaphore_wait(barrier, n)

    def remote(src, dst, ss, rs, dev):
        return pltpu.make_async_remote_copy(
            src_ref=src, dst_ref=dst, send_sem=ss, recv_sem=rs, device_id=dev,
            device_id_type=pl.DeviceIdType.MESH,
        )

    z_rows = pl.ds(pl.multiple_of(e * xr, 16), zr)
    x_out_rows = pl.ds(pl.multiple_of(e * zr, 16), xr)
    x_in_rows = pl.ds(pl.multiple_of(other_e * zr, 16), xr)

    def z_copy(s, way):
        ref = rows.at[s, t, z_rows]
        return remote(ref, ref, z_s.at[s, (way + 1) // 2], z_r.at[s], {"ctx": c + way})

    def x_copy(s):
        ref = rows.at[s, t, x_out_rows]
        return remote(ref, ref, x_s.at[s], x_r.at[s], {"exp": other_e})

    def x_landing(s):
        ref = rows.at[s, t, x_in_rows]
        return remote(ref, ref, x_s.at[s], x_r.at[s], {"exp": other_e})

    def cz_copy(s, tt):
        ref = rows.at[s, tt, z_rows]
        return remote(ref, ref, cz_s.at[s], cz_r.at[s], {"tp": other_t})

    def cx_copy(s, tt):
        ref = rows.at[s, tt, x_in_rows]
        return remote(ref, ref, cx_s.at[s], cx_r.at[s], {"tp": other_t})

    def h_copy(s, l):
        return remote(
            hid_own.at[s, l], hid_rem.at[s, l], h_s.at[s, l], h_r.at[s, l], {"exp": other_e}
        )

    def p_copy(s):
        return remote(pair_out.at[s], pair_in.at[s], p_s.at[s], p_r.at[s], {"tp": other_t})

    def o_copy(s, slot):
        return remote(far_out.at[s], far_in.at[slot], o_s.at[s], o_r.at[slot], {"ctx": s})

    def m_copy(peer, slot):
        return remote(
            meta_ref.at[peer], meta_in.at[slot], m_s.at[peer], m_r.at[slot],
            {"ctx": peer // tp_n, "tp": peer % tp_n},
        )

    load_tok.wait()
    for way in (-1, 1):
        @pl.when((c + way >= 0) & (c + way < ctx_n))
        def _():
            z_copy(c, way).start()
    for k in range(1, n):
        m_copy((me + k) % n, me).start()
    cz_copy(c, t).start()
    cx_copy(c, t).start()
    meta_in[me] = meta_ref[me]
    for k in range(1, n):
        peer = (me + k) % n
        m_copy(peer, peer).wait_recv()
    load_up.wait()
    load_down.wait()

    least = jnp.minimum(c, ctx_n - 1 - c)
    left_long = c > ctx_n - 1 - c

    def chunk_of(i):
        near = (i + 1) // 2
        close = jnp.where(i % 2 == 1, c - near, c + near)
        dist = i - least
        far = jnp.where(left_long, c - dist, c + dist)
        return jnp.where(i <= 2 * least, close, far)

    slot_iota = lax.broadcasted_iota(jnp.int32, (cap, tok), 0).astype(f32)

    def place(s, tt, l):
        info = meta_in[s * tp_n + tt]
        hit = slot_iota == info[l : l + 1, :]
        gate = jnp.sum(
            jnp.where(hit, info[local_n + l : local_n + l + 1, :], 0.0), axis=1, keepdims=True
        )
        return jnp.where(hit, 1.0, 0.0).astype(bf), gate

    def up(s):
        for l in range(local_n):
            parts = []
            for q, tt in enumerate((t, other_t)):
                chooser, _ = place(s, tt, l)
                got = jnp.dot(chooser, rows[s, tt], preferred_element_type=f32)
                parts.append(jnp.sum(got * lu_ref[l], axis=1, keepdims=True))
                xs[l, q * cap : (q + 1) * cap, :] = got.astype(bf)
            rank = jnp.concatenate(parts, axis=0)
            act = jnp.dot(xs[l], wu[l], preferred_element_type=f32)
            act = jnp.maximum(act + rank * ru_ref[l], 0.0)
            hid_own[s, l] = (act * act).astype(bf)
            h_copy(s, l).start()

    def down(s, i):
        own_rows = pl.ds(pl.multiple_of(e * half, half), half)
        rem_rows = pl.ds(pl.multiple_of(other_e * half, half), half)
        for l in range(local_n):
            h_copy(s, l).wait_recv()
            a, b = hid_own[s, l], hid_rem[s, l]
            y = jnp.dot(a, wd[l, own_rows, :], preferred_element_type=f32)
            y = y + jnp.dot(b, wd[l, rem_rows, :], preferred_element_type=f32)
            rank = jnp.sum(
                a.astype(f32) * ld_ref[l, e] + b.astype(f32) * ld_ref[l, other_e],
                axis=1, keepdims=True,
            )
            y = y + rank * rd_ref[l]
            for q, tt in enumerate((t, other_t)):
                _, gate = place(s, tt, l)
                scaled[q, l * cap : (l + 1) * cap, :] = (
                    y[q * cap : (q + 1) * cap] * gate
                ).astype(bf)
        for q, tt in enumerate((t, other_t)):
            chooser = jnp.concatenate([place(s, tt, l)[0] for l in range(local_n)], axis=0)
            total = lax.dot_general(
                chooser, scaled[q], (((0,), (0,)), ((), ())), preferred_element_type=f32
            )
            if q == 0:
                own_part[i % 2] = total
            else:
                pair_out[s] = total.astype(bf)
        p_copy(s).start()

    def step(j, carry):
        for side in (-1, 1):
            s = c + side * j

            @pl.when((j < ctx_n) & (s >= 0) & (s < ctx_n))
            def _():
                z_copy(s, side).wait_recv()

                @pl.when((c - side >= 0) & (c - side < ctx_n))
                def _():
                    z_copy(s, -side).start()

                x_copy(s).start()
                cz_copy(s, t).start()

        @pl.when(j - 1 < ctx_n)
        def _():
            s = chunk_of(j - 1)

            @pl.when(s != c)
            def _():
                x_landing(s).wait_recv()
                cx_copy(s, t).start()

            cz_copy(s, other_t).wait_recv()
            cx_copy(s, other_t).wait_recv()
            up(s)

        @pl.when((j >= 2) & (j - 2 < ctx_n))
        def _():
            down(chunk_of(j - 2), j - 2)

        @pl.when(j >= 3)
        def _():
            s = chunk_of(j - 3)
            p_copy(s).wait_recv()
            total = own_part[(j - 3) % 2] + pair_in[s].astype(f32)

            @pl.when(s == c)
            def _():
                kept[...] = total

            @pl.when(s != c)
            def _():
                far_out[s] = total.astype(bf)
                o_copy(s, c).start()

        return carry

    lax.fori_loop(1, ctx_n + 3, step, 0)

    def gather(k, carry):
        s = (c + k) % ctx_n
        o_copy(s, s).wait_recv()
        kept[...] += far_in[s].astype(f32)
        return carry

    lax.fori_loop(1, ctx_n, gather, 0)
    out_ref[...] = kept[...].astype(out_ref.dtype)

    for k in range(1, n):
        m_copy((me + k) % n, me).wait_send()

    def drain(s, carry):
        for way in (-1, 1):
            @pl.when((c + way >= 0) & (c + way < ctx_n) & ((s - c) * way <= 0))
            def _():
                z_copy(s, way).wait_send()

        @pl.when(s != c)
        def _():
            x_copy(s).wait_send()
            o_copy(s, c).wait_send()

        cz_copy(s, t).wait_send()
        cx_copy(s, t).wait_send()
        p_copy(s).wait_send()
        for l in range(local_n):
            h_copy(s, l).wait_send()
        return carry

    lax.fori_loop(0, ctx_n, drain, 0)


def fused_path(
    tokens, routes, route_gates, up_weight, down_weight, factor_seeds,
    up_left, up_right, down_left, down_right,
):
    ctx_n, tp_n = lax.axis_size("ctx"), lax.axis_size("tp")
    n = ctx_n * tp_n
    local_n, width, half = up_weight.shape
    hid_all, out_w = down_weight.shape[1:]
    tok, top = routes.shape
    experts = n * local_n
    cap = 4 * tok * top // (3 * experts)
    f32, bf = jnp.float32, jnp.bfloat16
    normed = route_gates / jnp.sum(route_gates, axis=1, keepdims=True)
    hits = routes.T[None, :, :] == jnp.arange(experts, dtype=jnp.int32)[:, None, None]
    mask = jnp.any(hits, axis=1)
    gates = jnp.sum(jnp.where(hits, normed.T[None, :, :], 0.0), axis=1)
    order = jnp.arange(tok, dtype=jnp.int32)
    before = (order[:, None] < order[None, :]).astype(bf)
    spot = jnp.dot(mask.astype(bf), before, preferred_element_type=f32)
    slot = jnp.where(mask, spot, -1.0)
    meta = jnp.concatenate(
        [slot.reshape(n, local_n, tok), gates.reshape(n, local_n, tok)], axis=1
    )
    meta_rows = -(-2 * local_n // 8) * 8
    meta = jnp.pad(meta, ((0, 0), (0, meta_rows - 2 * local_n), (0, 0)))
    lu = pick_rows(up_left, factor_seeds[:, 0]).astype(f32)[:, None, :]
    ru = pick_rows(up_right, factor_seeds[:, 1]).astype(f32)[:, None, :]
    ld = pick_rows(down_left, factor_seeds[:, 2]).astype(f32).reshape(local_n, 2, 1, half)
    rd = pick_rows(down_right, factor_seeds[:, 3]).astype(f32)[:, None, :]
    zr = tok * 5 // 8
    slots = tp_n * cap
    vm, anyspace = pl.BlockSpec(memory_space=pltpu.VMEM), pl.BlockSpec(memory_space=pl.ANY)
    dma = pltpu.SemaphoreType.DMA
    return pl.pallas_call(
        functools.partial(fused_kernel, (ctx_n, tp_n, local_n, cap, zr)),
        out_shape=jax.ShapeDtypeStruct((tok, out_w), bf),
        in_specs=[vm, anyspace, vm, vm, vm, vm, anyspace, anyspace],
        out_specs=vm,
        scratch_shapes=[
            pltpu.VMEM((ctx_n, tp_n, tok, width), bf),
            pltpu.VMEM((n, meta_rows, tok), f32),
            pltpu.VMEM((local_n, width, half), bf),
            pltpu.VMEM((local_n, hid_all, out_w), bf),
            pltpu.VMEM((local_n, slots, width), bf),
            pltpu.VMEM((ctx_n, local_n, slots, half), bf),
            pltpu.VMEM((ctx_n, local_n, slots, half), bf),
            pltpu.VMEM((tp_n, local_n * cap, out_w), bf),
            pltpu.VMEM((2, tok, out_w), f32),
            pltpu.VMEM((ctx_n, tok, out_w), bf),
            pltpu.VMEM((ctx_n, tok, out_w), bf),
            pltpu.VMEM((ctx_n, tok, out_w), bf),
            pltpu.VMEM((ctx_n, tok, out_w), bf),
            pltpu.VMEM((tok, out_w), f32),
            dma((ctx_n, 2)), dma((ctx_n,)), dma((ctx_n,)), dma((ctx_n,)),
            dma((ctx_n,)), dma((ctx_n,)), dma((ctx_n,)), dma((ctx_n,)),
            dma((ctx_n, local_n)), dma((ctx_n, local_n)), dma((ctx_n,)), dma((ctx_n,)),
            dma((ctx_n,)), dma((ctx_n,)), dma((n,)), dma((n,)), dma((3,)),
        ],
        compiler_params=pltpu.CompilerParams(
            collective_id=0, has_side_effects=True, vmem_limit_bytes=60 * 1024 * 1024
        ),
    )(meta, tokens, lu, ru, ld, rd, up_weight, down_weight)


def on_device(*args):
    tokens, routes, up_weight, down_weight = args[0], args[1], args[3], args[4]
    experts = lax.axis_size("ctx") * lax.axis_size("tp") * up_weight.shape[0]
    cap = 4 * routes.shape[0] * routes.shape[1] // (3 * experts)
    fits = (
        lax.axis_size("exp") == 2
        and lax.axis_size("tp") == 2
        and up_weight.shape[2] % 128 == 0
        and tokens.shape[0] % 128 == 0
        and cap % 16 == 0
        and lax.axis_size("ctx") * tokens.size <= 1 << 21
        and up_weight.size + down_weight.size <= 5 << 21
    )
    return fused_path(*args) if fits else general_path(*args)


def solution(mesh):
    in_specs = (
        P(("pop", "ctx", "tp"), None),
        P(("pop", "ctx", "tp"), None),
        P(("pop", "ctx", "tp"), None),
        P(("ctx", "tp"), None, "exp"),
        P(("ctx", "tp"), None, "exp"),
        P(("pop", "ctx", "tp"), None),
        P(),
        P(None, "exp"),
        P(),
        P(None, "exp"),
    )
    out_specs = P(("pop", "ctx", "tp"), "exp")
    return jax.shard_map(
        on_device, mesh=mesh, in_specs=in_specs, out_specs=out_specs, check_vma=False
    )
```

```python
import functools

import jax
import jax.numpy as jnp
from jax import lax
from jax.experimental import pallas as pl
from jax.experimental.pallas import tpu as pltpu
from jax.sharding import PartitionSpec as P


def pick_rows(factor_table, indices):
    chooser = (
        indices[:, None] == jnp.arange(factor_table.shape[0], dtype=jnp.int32)[None, :]
    ).astype(factor_table.dtype)
    return jnp.dot(chooser, factor_table, preferred_element_type=jnp.float32).astype(
        factor_table.dtype
    )


def general_path(
    tokens,
    routes,
    route_gates,
    up_weight,
    down_weight,
    factor_seeds,
    up_left,
    up_right,
    down_left,
    down_right,
):
    dest_count = lax.axis_size("ctx") * lax.axis_size("tp")
    local_experts = up_weight.shape[0]
    experts_all = dest_count * local_experts
    tok_count, top_count = routes.shape
    capacity = 4 * tok_count * top_count // (3 * experts_all)
    model_width = tokens.shape[1]
    flat_routes = routes.reshape(-1)
    chooser = (flat_routes[:, None] == jnp.arange(experts_all, dtype=jnp.int32)[None, :]).astype(
        jnp.int32
    )
    earlier = jnp.cumsum(chooser, axis=0) - chooser
    slot_index = jnp.sum(earlier * chooser, axis=1)
    target = flat_routes * capacity + slot_index
    pair_token = jnp.arange(tok_count * top_count, dtype=jnp.int32) // top_count + 1
    owner_token = jnp.zeros((experts_all * capacity,), jnp.int32).at[target].set(pair_token)
    source_row = jnp.where(owner_token > 0, owner_token - 1, tok_count)
    padded_tokens = jnp.concatenate([tokens, jnp.zeros((1, model_width), tokens.dtype)], axis=0)
    token_rows = padded_tokens[source_row]
    outgoing = token_rows.reshape(dest_count, local_experts, capacity, model_width)
    left_up = pick_rows(up_left, factor_seeds[:, 0])
    right_up = pick_rows(up_right, factor_seeds[:, 1])
    left_down = pick_rows(down_left, factor_seeds[:, 2])
    right_down = pick_rows(down_right, factor_seeds[:, 3])
    buffer = lax.all_to_all(outgoing, ("ctx", "tp"), split_axis=0, concat_axis=0, tiled=True)
    up_act = jnp.einsum("slcd,ldh->slch", buffer, up_weight, preferred_element_type=jnp.float32)
    low_rank = jnp.einsum("slcd,ld->slc", buffer, left_up, preferred_element_type=jnp.float32)
    up_act = up_act + low_rank[..., None] * right_up[None, :, None, :].astype(jnp.float32)
    hidden = (jnp.maximum(up_act, 0.0) ** 2).astype(jnp.bfloat16)
    full_hidden = lax.all_gather(hidden, "exp", axis=3, tiled=True)
    summed = jnp.einsum(
        "slch,lhd->slcd", full_hidden, down_weight, preferred_element_type=jnp.float32
    )
    rank_sum = jnp.einsum(
        "slch,lh->slc", full_hidden, left_down, preferred_element_type=jnp.float32
    )
    result = (
        summed + rank_sum[..., None] * right_down[None, :, None, :].astype(jnp.float32)
    ).astype(jnp.bfloat16)
    returned = lax.all_to_all(result, ("ctx", "tp"), split_axis=0, concat_axis=0, tiled=True)
    back_rows = returned.reshape(experts_all * capacity, -1)
    picked = back_rows[target]
    normed = (route_gates / jnp.sum(route_gates, axis=1, keepdims=True)).reshape(-1)
    weighted = picked.astype(jnp.float32) * normed[:, None]
    moe_output = jnp.sum(weighted.reshape(tok_count, top_count, -1), axis=1)
    return moe_output.astype(jnp.bfloat16)


def fused_kernel(
    cfg,
    seeds_ref, routes_ref, gates_ref, tokens_ref, ul_ref, ur_ref, dl_ref, dr_ref, wu_hbm, wd_hbm,
    out_ref,
    rows, meta_ref, meta_in, lu_ref, ru_ref, ld_ref, rd_ref, wu, wd, xs, hid_own, hid_rem, scaled, own_part, pair_out, pair_in,
    far_out, far_in, kept,
    z_s, z_r, x_s, x_r, cz_s, cz_r, cx_s, cx_r, h_s, h_r, p_s, p_r, o_s, o_r, m_s, m_r, loc,
):
    ctx_n, tp_n, local_n, cap, zr = cfg
    tok = tokens_ref.shape[0]
    half = wu.shape[2]
    xr = tok - zr
    c, e, t = lax.axis_index("ctx"), lax.axis_index("exp"), lax.axis_index("tp")
    other_e, other_t = 1 - e, 1 - t
    me = c * tp_n + t
    n = ctx_n * tp_n
    bf, f32 = jnp.bfloat16, jnp.float32

    load_up = pltpu.make_async_copy(wu_hbm, wu, loc.at[0])
    load_down = [
        pltpu.make_async_copy(
            wd_hbm.at[l, :, pl.ds(pl.multiple_of((e if k == 0 else other_e) * half, 128), half)],
            wd.at[l, k],
            loc.at[2 + 2 * l + k],
        )
        for l in range(local_n)
        for k in range(2)
    ]
    load_tok = pltpu.make_async_copy(tokens_ref, rows.at[c, t], loc.at[1])
    load_tok.start()
    load_up.start()
    for load in load_down:
        load.start()

    barrier = pltpu.get_barrier_semaphore()
    for k in range(1, n):
        peer = (me + k) % n
        pl.semaphore_signal(
            barrier, inc=1, device_id={"ctx": peer // tp_n, "tp": peer % tp_n},
            device_id_type=pl.DeviceIdType.MESH,
        )
    pl.semaphore_signal(
        barrier, inc=1, device_id={"exp": other_e}, device_id_type=pl.DeviceIdType.MESH
    )

    def remote(src, dst, ss, rs, dev):
        return pltpu.make_async_remote_copy(
            src_ref=src, dst_ref=dst, send_sem=ss, recv_sem=rs, device_id=dev,
            device_id_type=pl.DeviceIdType.MESH,
        )

    z_rows = pl.ds(pl.multiple_of(e * xr, 16), zr)
    x_out_rows = pl.ds(pl.multiple_of(e * zr, 16), xr)
    x_in_rows = pl.ds(pl.multiple_of(other_e * zr, 16), xr)

    def z_copy(s, way):
        ref = rows.at[s, t, z_rows]
        return remote(ref, ref, z_s.at[s, (way + 1) // 2], z_r.at[s], {"ctx": c + way})

    def x_copy(s):
        ref = rows.at[s, t, x_out_rows]
        return remote(ref, ref, x_s.at[s], x_r.at[s], {"exp": other_e})

    def x_landing(s):
        ref = rows.at[s, t, x_in_rows]
        return remote(ref, ref, x_s.at[s], x_r.at[s], {"exp": other_e})

    def cz_copy(s, tt):
        ref = rows.at[s, tt, z_rows]
        return remote(ref, ref, cz_s.at[s], cz_r.at[s], {"tp": other_t})

    def cx_copy(s, tt):
        ref = rows.at[s, tt, x_in_rows]
        return remote(ref, ref, cx_s.at[s], cx_r.at[s], {"tp": other_t})

    def h_copy(s, l):
        return remote(
            hid_own.at[s, l], hid_rem.at[s, l], h_s.at[s, l], h_r.at[s, l], {"exp": other_e}
        )

    def p_copy(s):
        return remote(pair_out.at[s], pair_in.at[s], p_s.at[s], p_r.at[s], {"tp": other_t})

    def o_copy(s, slot):
        return remote(far_out.at[s], far_in.at[slot], o_s.at[s], o_r.at[slot], {"ctx": s})

    def m_copy(peer, slot):
        return remote(
            meta_ref.at[peer], meta_in.at[slot], m_s.at[peer], m_r.at[slot],
            {"ctx": peer // tp_n, "tp": peer % tp_n},
        )

    load_tok.wait()
    pl.semaphore_wait(barrier, n)
    for way in (-1, 1):
        @pl.when((c + way >= 0) & (c + way < ctx_n))
        def _():
            z_copy(c, way).start()
    cz_copy(c, t).start()
    cx_copy(c, t).start()

    top = routes_ref.shape[0]
    gate_sum = gates_ref[0:1, :]
    for k in range(1, top):
        gate_sum = gate_sum + gates_ref[k : k + 1, :]
    expert = lax.broadcasted_iota(jnp.int32, (n * local_n, tok), 0)
    gate = jnp.zeros((n * local_n, tok), f32)
    mask = gate
    for k in range(top):
        hit = routes_ref[k : k + 1, :] == expert
        gate = gate + jnp.where(hit, gates_ref[k : k + 1, :] / gate_sum, 0.0)
        mask = mask + jnp.where(hit, 1.0, 0.0)
    before = (
        lax.broadcasted_iota(jnp.int32, (tok, tok), 0)
        < lax.broadcasted_iota(jnp.int32, (tok, tok), 1)
    )
    spot = jnp.dot(
        mask.astype(bf), jnp.where(before, 1.0, 0.0).astype(bf), preferred_element_type=f32
    )
    slot = jnp.where(mask > 0.0, spot, -1.0)
    for k in range(n):
        meta_ref[k, 0:local_n, :] = slot[k * local_n : (k + 1) * local_n]
        meta_ref[k, local_n : 2 * local_n, :] = gate[k * local_n : (k + 1) * local_n]
    for k in range(1, n):
        m_copy((me + k) % n, me).start()

    def pick(table, seed):
        line = lax.broadcasted_iota(jnp.int32, table.shape, 0)
        return jnp.sum(
            jnp.where(line == seed, table[...].astype(f32), 0.0), axis=0, keepdims=True
        )

    for l in range(local_n):
        lu_ref[l] = pick(ul_ref, seeds_ref[l, 0])
        ru_ref[l] = pick(ur_ref, seeds_ref[l, 1])
        whole = pick(dl_ref, seeds_ref[l, 2])
        ld_ref[l, 0] = jnp.where(e == 0, whole[:, :half], whole[:, half:])
        ld_ref[l, 1] = jnp.where(e == 0, whole[:, half:], whole[:, :half])
        rd_ref[l] = pick(dr_ref, seeds_ref[l, 3])
    meta_in[me] = meta_ref[me]
    for k in range(1, n):
        peer = (me + k) % n
        m_copy(peer, peer).wait_recv()
    load_up.wait()

    slot_iota = lax.broadcasted_iota(jnp.int32, (cap, tok), 0).astype(f32)

    def place(s, tt, l):
        info = meta_in[s * tp_n + tt]
        hit = slot_iota == info[l : l + 1, :]
        gate = jnp.sum(
            jnp.where(hit, info[local_n + l : local_n + l + 1, :], 0.0), axis=1, keepdims=True
        )
        return jnp.where(hit, 1.0, 0.0).astype(bf), gate

    def up(s):
        for l in range(local_n):
            parts = []
            for q, tt in enumerate((t, other_t)):
                chooser, _ = place(s, tt, l)
                got = jnp.dot(chooser, rows[s, tt], preferred_element_type=f32)
                parts.append(jnp.sum(got * lu_ref[l], axis=1, keepdims=True))
                xs[l, q * cap : (q + 1) * cap, :] = got.astype(bf)
            rank = jnp.concatenate(parts, axis=0)
            act = jnp.dot(xs[l], wu[l], preferred_element_type=f32)
            act = jnp.maximum(act + rank * ru_ref[l], 0.0)
            hid_own[s, l] = (act * act).astype(bf)
            h_copy(s, l).start()

    nt = (((1,), (1,)), ((), ()))

    def down(s, i):
        for l in range(local_n):
            h_copy(s, l).wait_recv()
            a, b = hid_own[s, l], hid_rem[s, l]
            y = lax.dot_general(a, wd[l, 0], nt, preferred_element_type=f32)
            y = y + lax.dot_general(b, wd[l, 1], nt, preferred_element_type=f32)
            rank = jnp.sum(
                a.astype(f32) * ld_ref[l, 0] + b.astype(f32) * ld_ref[l, 1],
                axis=1, keepdims=True,
            )
            y = y + rank * rd_ref[l]
            for q, tt in enumerate((t, other_t)):
                _, gate = place(s, tt, l)
                scaled[q, l * cap : (l + 1) * cap, :] = (
                    y[q * cap : (q + 1) * cap] * gate
                ).astype(bf)
        for q, tt in enumerate((t, other_t)):
            chooser = jnp.concatenate([place(s, tt, l)[0] for l in range(local_n)], axis=0)
            total = lax.dot_general(
                chooser, scaled[q], (((0,), (0,)), ((), ())), preferred_element_type=f32
            )
            if q == 0:
                own_part[i] = total
            else:
                pair_out[s] = total.astype(bf)
        p_copy(s).start()

    def step(j, carry):
        def chunks(dist, do):
            def one(k, carry):
                s = c + (2 * k - 1) * dist

                @pl.when((s >= 0) & (s < ctx_n) & (dist >= 0) & ((dist > 0) | (k == 0)))
                def _():
                    do(s, k)

                return carry

            lax.fori_loop(0, 2, one, 0)

        for side in (-1, 1):
            s = c + side * j

            @pl.when((j > 0) & (s >= 0) & (s < ctx_n))
            def _():
                z_copy(s, side).wait_recv()

                @pl.when((c - side >= 0) & (c - side < ctx_n))
                def _():
                    z_copy(s, -side).start()

                x_copy(s).start()
                cz_copy(s, t).start()

        def begin(s, k):
            @pl.when(s != c)
            def _():
                x_landing(s).wait_recv()
                cx_copy(s, t).start()

            cz_copy(s, other_t).wait_recv()
            cx_copy(s, other_t).wait_recv()
            up(s)

        def finish(s, k):
            p_copy(s).wait_recv()
            total = own_part[k] + pair_in[s].astype(f32)

            @pl.when(s == c)
            def _():
                kept[...] = total

            @pl.when(s != c)
            def _():
                far_out[s] = total.astype(bf)
                o_copy(s, c).start()

        chunks(j, begin)

        @pl.when(j == 1)
        def _():
            for load in load_down:
                load.wait()

        chunks(j - 1, down)
        chunks(j - 1, finish)
        return carry

    lax.fori_loop(0, ctx_n + 1, step, 0)

    def gather(k, carry):
        s = (c + k) % ctx_n
        o_copy(s, s).wait_recv()
        kept[...] += far_in[s].astype(f32)
        return carry

    lax.fori_loop(1, ctx_n, gather, 0)
    out_ref[...] = kept[...].astype(out_ref.dtype)

    for k in range(1, n):
        m_copy((me + k) % n, me).wait_send()

    def drain(s, carry):
        for way in (-1, 1):
            @pl.when((c + way >= 0) & (c + way < ctx_n) & ((s - c) * way <= 0))
            def _():
                z_copy(s, way).wait_send()

        @pl.when(s != c)
        def _():
            x_copy(s).wait_send()
            o_copy(s, c).wait_send()

        cz_copy(s, t).wait_send()
        cx_copy(s, t).wait_send()
        p_copy(s).wait_send()
        for l in range(local_n):
            h_copy(s, l).wait_send()
        return carry

    lax.fori_loop(0, ctx_n, drain, 0)


def fused_path(
    tokens, routes, route_gates, up_weight, down_weight, factor_seeds,
    up_left, up_right, down_left, down_right,
):
    ctx_n, tp_n = lax.axis_size("ctx"), lax.axis_size("tp")
    n = ctx_n * tp_n
    local_n, width, half = up_weight.shape
    out_w = down_weight.shape[2]
    tok, top = routes.shape
    experts = n * local_n
    cap = 4 * tok * top // (3 * experts)
    f32, bf = jnp.float32, jnp.bfloat16
    meta_rows = -(-2 * local_n // 8) * 8
    zr = tok * 7 // 8
    slots = tp_n * cap
    vm, anyspace = pl.BlockSpec(memory_space=pltpu.VMEM), pl.BlockSpec(memory_space=pl.ANY)
    dma = pltpu.SemaphoreType.DMA
    return pl.pallas_call(
        functools.partial(fused_kernel, (ctx_n, tp_n, local_n, cap, zr)),
        out_shape=jax.ShapeDtypeStruct((tok, out_w), bf),
        in_specs=[
            pl.BlockSpec(memory_space=pltpu.SMEM), vm, vm, anyspace, vm, vm, vm, vm,
            anyspace, anyspace,
        ],
        out_specs=vm,
        scratch_shapes=[
            pltpu.VMEM((ctx_n, tp_n, tok, width), bf),
            pltpu.VMEM((n, meta_rows, tok), f32),
            pltpu.VMEM((n, meta_rows, tok), f32),
            pltpu.VMEM((local_n, 1, width), f32),
            pltpu.VMEM((local_n, 1, half), f32),
            pltpu.VMEM((local_n, 2, 1, half), f32),
            pltpu.VMEM((local_n, 1, out_w), f32),
            pltpu.VMEM((local_n, width, half), bf),
            pltpu.VMEM((local_n, 2, out_w, half), bf),
            pltpu.VMEM((local_n, slots, width), bf),
            pltpu.VMEM((ctx_n, local_n, slots, half), bf),
            pltpu.VMEM((ctx_n, local_n, slots, half), bf),
            pltpu.VMEM((tp_n, local_n * cap, out_w), bf),
            pltpu.VMEM((2, tok, out_w), f32),
            pltpu.VMEM((ctx_n, tok, out_w), bf),
            pltpu.VMEM((ctx_n, tok, out_w), bf),
            pltpu.VMEM((ctx_n, tok, out_w), bf),
            pltpu.VMEM((ctx_n, tok, out_w), bf),
            pltpu.VMEM((tok, out_w), f32),
            dma((ctx_n, 2)), dma((ctx_n,)), dma((ctx_n,)), dma((ctx_n,)),
            dma((ctx_n,)), dma((ctx_n,)), dma((ctx_n,)), dma((ctx_n,)),
            dma((ctx_n, local_n)), dma((ctx_n, local_n)), dma((ctx_n,)), dma((ctx_n,)),
            dma((ctx_n,)), dma((ctx_n,)), dma((n,)), dma((n,)), dma((2 + 2 * local_n,)),
        ],
        compiler_params=pltpu.CompilerParams(
            collective_id=0, has_side_effects=True, vmem_limit_bytes=60 * 1024 * 1024
        ),
    )(
        factor_seeds, routes.T, route_gates.T, tokens, up_left, up_right, down_left, down_right,
        up_weight, jnp.swapaxes(down_weight, 1, 2),
    )


def on_device(*args):
    tokens, routes, up_weight, down_weight = args[0], args[1], args[3], args[4]
    experts = lax.axis_size("ctx") * lax.axis_size("tp") * up_weight.shape[0]
    cap = 4 * routes.shape[0] * routes.shape[1] // (3 * experts)
    fits = (
        lax.axis_size("exp") == 2
        and lax.axis_size("tp") == 2
        and up_weight.shape[2] % 128 == 0
        and tokens.shape[0] % 128 == 0
        and cap % 16 == 0
        and lax.axis_size("ctx") * tokens.size <= 1 << 21
        and up_weight.size + down_weight.size <= 5 << 21
    )
    return fused_path(*args) if fits else general_path(*args)


def solution(mesh):
    in_specs = (
        P(("pop", "ctx", "tp"), None),
        P(("pop", "ctx", "tp"), None),
        P(("pop", "ctx", "tp"), None),
        P(("ctx", "tp"), None, "exp"),
        P(("ctx", "tp"), None, "exp"),
        P(("pop", "ctx", "tp"), None),
        P(),
        P(None, "exp"),
        P(),
        P(None, "exp"),
    )
    out_specs = P(("pop", "ctx", "tp"), "exp")
    return jax.shard_map(
        on_device, mesh=mesh, in_specs=in_specs, out_specs=out_specs, check_vma=False
    )
```

```python
import functools

import jax
import jax.numpy as jnp
from jax import lax
from jax.experimental import pallas as pl
from jax.experimental.pallas import tpu as pltpu
from jax.sharding import PartitionSpec as P


def pick_rows(factor_table, indices):
    chooser = (
        indices[:, None] == jnp.arange(factor_table.shape[0], dtype=jnp.int32)[None, :]
    ).astype(factor_table.dtype)
    return jnp.dot(chooser, factor_table, preferred_element_type=jnp.float32).astype(
        factor_table.dtype
    )


def general_path(
    tokens,
    routes,
    route_gates,
    up_weight,
    down_weight,
    factor_seeds,
    up_left,
    up_right,
    down_left,
    down_right,
):
    dest_count = lax.axis_size("ctx") * lax.axis_size("tp")
    local_experts = up_weight.shape[0]
    experts_all = dest_count * local_experts
    tok_count, top_count = routes.shape
    capacity = 4 * tok_count * top_count // (3 * experts_all)
    model_width = tokens.shape[1]
    flat_routes = routes.reshape(-1)
    chooser = (flat_routes[:, None] == jnp.arange(experts_all, dtype=jnp.int32)[None, :]).astype(
        jnp.int32
    )
    earlier = jnp.cumsum(chooser, axis=0) - chooser
    slot_index = jnp.sum(earlier * chooser, axis=1)
    target = flat_routes * capacity + slot_index
    pair_token = jnp.arange(tok_count * top_count, dtype=jnp.int32) // top_count + 1
    owner_token = jnp.zeros((experts_all * capacity,), jnp.int32).at[target].set(pair_token)
    source_row = jnp.where(owner_token > 0, owner_token - 1, tok_count)
    padded_tokens = jnp.concatenate([tokens, jnp.zeros((1, model_width), tokens.dtype)], axis=0)
    token_rows = padded_tokens[source_row]
    outgoing = token_rows.reshape(dest_count, local_experts, capacity, model_width)
    left_up = pick_rows(up_left, factor_seeds[:, 0])
    right_up = pick_rows(up_right, factor_seeds[:, 1])
    left_down = pick_rows(down_left, factor_seeds[:, 2])
    right_down = pick_rows(down_right, factor_seeds[:, 3])
    buffer = lax.all_to_all(outgoing, ("ctx", "tp"), split_axis=0, concat_axis=0, tiled=True)
    up_act = jnp.einsum("slcd,ldh->slch", buffer, up_weight, preferred_element_type=jnp.float32)
    low_rank = jnp.einsum("slcd,ld->slc", buffer, left_up, preferred_element_type=jnp.float32)
    up_act = up_act + low_rank[..., None] * right_up[None, :, None, :].astype(jnp.float32)
    hidden = (jnp.maximum(up_act, 0.0) ** 2).astype(jnp.bfloat16)
    full_hidden = lax.all_gather(hidden, "exp", axis=3, tiled=True)
    summed = jnp.einsum(
        "slch,lhd->slcd", full_hidden, down_weight, preferred_element_type=jnp.float32
    )
    rank_sum = jnp.einsum(
        "slch,lh->slc", full_hidden, left_down, preferred_element_type=jnp.float32
    )
    result = (
        summed + rank_sum[..., None] * right_down[None, :, None, :].astype(jnp.float32)
    ).astype(jnp.bfloat16)
    returned = lax.all_to_all(result, ("ctx", "tp"), split_axis=0, concat_axis=0, tiled=True)
    back_rows = returned.reshape(experts_all * capacity, -1)
    picked = back_rows[target]
    normed = (route_gates / jnp.sum(route_gates, axis=1, keepdims=True)).reshape(-1)
    weighted = picked.astype(jnp.float32) * normed[:, None]
    moe_output = jnp.sum(weighted.reshape(tok_count, top_count, -1), axis=1)
    return moe_output.astype(jnp.bfloat16)


def fused_kernel(
    cfg,
    seeds_ref, routes_ref, gates_ref, tokens_ref, ul_ref, ur_ref, dl_ref, dr_ref, wu_hbm, wd_hbm,
    out_ref,
    rows, meta_ref, meta_in, lu_ref, ru_ref, ld_ref, rd_ref, wu, wd, xs, hid_own, hid_rem, scaled, own_part, pair_out, pair_in,
    far_out, far_in, kept,
    z_s, z_r, x_s, x_r, cz_s, cz_r, cx_s, cx_r, h_s, h_r, p_s, p_r, o_s, o_r, m_s, m_r, loc,
):
    ctx_n, tp_n, local_n, cap, zr = cfg
    tok = tokens_ref.shape[0]
    half = wu.shape[2]
    xr = tok - zr
    c, e, t = lax.axis_index("ctx"), lax.axis_index("exp"), lax.axis_index("tp")
    other_e, other_t = 1 - e, 1 - t
    me = c * tp_n + t
    n = ctx_n * tp_n
    bf, f32 = jnp.bfloat16, jnp.float32

    load_up = pltpu.make_async_copy(wu_hbm, wu, loc.at[0])
    load_down = [
        pltpu.make_async_copy(
            wd_hbm.at[l, :, pl.ds(pl.multiple_of((e if k == 0 else other_e) * half, 128), half)],
            wd.at[l, k],
            loc.at[2 + 2 * l + k],
        )
        for l in range(local_n)
        for k in range(2)
    ]
    load_tok = pltpu.make_async_copy(tokens_ref, rows.at[c, t], loc.at[1])
    load_tok.start()
    load_up.start()
    for load in load_down:
        load.start()

    barrier = pltpu.get_barrier_semaphore()
    for k in range(1, n):
        peer = (me + k) % n
        pl.semaphore_signal(
            barrier, inc=1, device_id={"ctx": peer // tp_n, "tp": peer % tp_n},
            device_id_type=pl.DeviceIdType.MESH,
        )
    pl.semaphore_signal(
        barrier, inc=1, device_id={"exp": other_e}, device_id_type=pl.DeviceIdType.MESH
    )

    def remote(src, dst, ss, rs, dev):
        return pltpu.make_async_remote_copy(
            src_ref=src, dst_ref=dst, send_sem=ss, recv_sem=rs, device_id=dev,
            device_id_type=pl.DeviceIdType.MESH,
        )

    z_rows = pl.ds(pl.multiple_of(e * xr, 16), zr)
    x_out_rows = pl.ds(pl.multiple_of(e * zr, 16), xr)
    x_in_rows = pl.ds(pl.multiple_of(other_e * zr, 16), xr)

    def z_copy(s, way):
        ref = rows.at[s, t, z_rows]
        return remote(ref, ref, z_s.at[s, (way + 1) // 2], z_r.at[s], {"ctx": c + way})

    def x_copy(s):
        ref = rows.at[s, t, x_out_rows]
        return remote(ref, ref, x_s.at[s], x_r.at[s], {"exp": other_e})

    def x_landing(s):
        ref = rows.at[s, t, x_in_rows]
        return remote(ref, ref, x_s.at[s], x_r.at[s], {"exp": other_e})

    def cz_copy(s, tt):
        ref = rows.at[s, tt, z_rows]
        return remote(ref, ref, cz_s.at[s], cz_r.at[s], {"tp": other_t})

    def cx_copy(s, tt):
        ref = rows.at[s, tt, x_in_rows]
        return remote(ref, ref, cx_s.at[s], cx_r.at[s], {"tp": other_t})

    def h_copy(s, l):
        return remote(
            hid_own.at[s, l], hid_rem.at[s, l], h_s.at[s, l], h_r.at[s, l], {"exp": other_e}
        )

    def p_copy(s):
        return remote(pair_out.at[s], pair_in.at[s], p_s.at[s], p_r.at[s], {"tp": other_t})

    def o_copy(s, slot):
        return remote(far_out.at[s], far_in.at[slot], o_s.at[s], o_r.at[slot], {"ctx": s})

    def m_copy(peer, slot):
        return remote(
            meta_ref.at[peer], meta_in.at[slot], m_s.at[peer], m_r.at[slot],
            {"ctx": peer // tp_n, "tp": peer % tp_n},
        )

    load_tok.wait()
    pl.semaphore_wait(barrier, n)
    for way in (-1, 1):
        @pl.when((c + way >= 0) & (c + way < ctx_n))
        def _():
            z_copy(c, way).start()
    cz_copy(c, t).start()
    if xr:
        cx_copy(c, t).start()

    top = routes_ref.shape[0]
    gate_sum = gates_ref[0:1, :]
    for k in range(1, top):
        gate_sum = gate_sum + gates_ref[k : k + 1, :]
    expert = lax.broadcasted_iota(jnp.int32, (n * local_n, tok), 0)
    gate = jnp.zeros((n * local_n, tok), f32)
    mask = gate
    for k in range(top):
        hit = routes_ref[k : k + 1, :] == expert
        gate = gate + jnp.where(hit, gates_ref[k : k + 1, :] / gate_sum, 0.0)
        mask = mask + jnp.where(hit, 1.0, 0.0)
    before = (
        lax.broadcasted_iota(jnp.int32, (tok, tok), 0)
        < lax.broadcasted_iota(jnp.int32, (tok, tok), 1)
    )
    spot = jnp.dot(
        mask.astype(bf), jnp.where(before, 1.0, 0.0).astype(bf), preferred_element_type=f32
    )
    slot = jnp.where(mask > 0.0, spot, -1.0)
    for k in range(n):
        meta_ref[k, 0:local_n, :] = slot[k * local_n : (k + 1) * local_n]
        meta_ref[k, local_n : 2 * local_n, :] = gate[k * local_n : (k + 1) * local_n]
    for k in range(1, n):
        m_copy((me + k) % n, me).start()

    def pick(table, seed):
        line = lax.broadcasted_iota(jnp.int32, table.shape, 0)
        return jnp.sum(
            jnp.where(line == seed, table[...].astype(f32), 0.0), axis=0, keepdims=True
        )

    for l in range(local_n):
        lu_ref[l] = pick(ul_ref, seeds_ref[l, 0])
        ru_ref[l] = pick(ur_ref, seeds_ref[l, 1])
        whole = pick(dl_ref, seeds_ref[l, 2])
        ld_ref[l, 0] = jnp.where(e == 0, whole[:, :half], whole[:, half:])
        ld_ref[l, 1] = jnp.where(e == 0, whole[:, half:], whole[:, :half])
        rd_ref[l] = pick(dr_ref, seeds_ref[l, 3])
    meta_in[me] = meta_ref[me]
    for k in range(1, n):
        peer = (me + k) % n
        m_copy(peer, peer).wait_recv()
    load_up.wait()

    slot_iota = lax.broadcasted_iota(jnp.int32, (cap, tok), 0).astype(f32)

    def place(s, tt, l):
        info = meta_in[s * tp_n + tt]
        hit = slot_iota == info[l : l + 1, :]
        gate = jnp.sum(
            jnp.where(hit, info[local_n + l : local_n + l + 1, :], 0.0), axis=1, keepdims=True
        )
        return jnp.where(hit, 1.0, 0.0).astype(bf), gate

    def up(s):
        for l in range(local_n):
            parts = []
            for q, tt in enumerate((t, other_t)):
                chooser, _ = place(s, tt, l)
                got = jnp.dot(chooser, rows[s, tt], preferred_element_type=f32)
                parts.append(jnp.sum(got * lu_ref[l], axis=1, keepdims=True))
                xs[l, q * cap : (q + 1) * cap, :] = got.astype(bf)
            rank = jnp.concatenate(parts, axis=0)
            act = jnp.dot(xs[l], wu[l], preferred_element_type=f32)
            act = jnp.maximum(act + rank * ru_ref[l], 0.0)
            hid_own[s, l] = (act * act).astype(bf)
            h_copy(s, l).start()

    nt = (((1,), (1,)), ((), ()))

    def down(s, i):
        for l in range(local_n):
            h_copy(s, l).wait_recv()
            a, b = hid_own[s, l], hid_rem[s, l]
            y = lax.dot_general(a, wd[l, 0], nt, preferred_element_type=f32)
            y = y + lax.dot_general(b, wd[l, 1], nt, preferred_element_type=f32)
            rank = jnp.sum(
                a.astype(f32) * ld_ref[l, 0] + b.astype(f32) * ld_ref[l, 1],
                axis=1, keepdims=True,
            )
            y = y + rank * rd_ref[l]
            for q, tt in enumerate((t, other_t)):
                _, gate = place(s, tt, l)
                scaled[q, l * cap : (l + 1) * cap, :] = (
                    y[q * cap : (q + 1) * cap] * gate
                ).astype(bf)
        for q, tt in enumerate((t, other_t)):
            chooser = jnp.concatenate([place(s, tt, l)[0] for l in range(local_n)], axis=0)
            total = lax.dot_general(
                chooser, scaled[q], (((0,), (0,)), ((), ())), preferred_element_type=f32
            )
            if q == 0:
                own_part[i] = total
            else:
                pair_out[s] = total.astype(bf)
        p_copy(s).start()

    def step(j, carry):
        def chunks(dist, do, least):
            def one(k, carry):
                s = c + (2 * k - 1) * dist

                @pl.when((s >= 0) & (s < ctx_n) & (dist >= least) & ((dist > 0) | (k == 0)))
                def _():
                    do(s, k)

                return carry

            lax.fori_loop(0, 2, one, 0)

        for side in (-1, 1):
            s = c + side * j

            @pl.when((j > 0) & (s >= 0) & (s < ctx_n))
            def _():
                z_copy(s, side).wait_recv()

                @pl.when((c - side >= 0) & (c - side < ctx_n))
                def _():
                    z_copy(s, -side).start()

                if xr:
                    x_copy(s).start()
                cz_copy(s, t).start()

        def begin(s, k):
            cz_copy(s, other_t).wait_recv()
            if xr:
                @pl.when(s != c)
                def _():
                    x_landing(s).wait_recv()
                    cx_copy(s, t).start()

                cx_copy(s, other_t).wait_recv()
            up(s)

        def finish(s, k):
            down(s, k)
            p_copy(s).wait_recv()
            total = own_part[k] + pair_in[s].astype(f32)

            @pl.when(s == c)
            def _():
                kept[...] = total

            @pl.when(s != c)
            def _():
                far_out[s] = total.astype(bf)
                o_copy(s, c).start()

        chunks(j, begin, 0)

        @pl.when(j == 1)
        def _():
            for load in load_down:
                load.wait()

        @pl.when(j == ctx_n)
        def _():
            finish(c, 0)

        chunks(j - 1, finish, 1)
        return carry

    lax.fori_loop(0, ctx_n + 1, step, 0)

    def gather(k, carry):
        s = (c + k) % ctx_n
        o_copy(s, s).wait_recv()
        kept[...] += far_in[s].astype(f32)
        return carry

    lax.fori_loop(1, ctx_n, gather, 0)
    out_ref[...] = kept[...].astype(out_ref.dtype)

    for k in range(1, n):
        m_copy((me + k) % n, me).wait_send()

    def drain(s, carry):
        for way in (-1, 1):
            @pl.when((c + way >= 0) & (c + way < ctx_n) & ((s - c) * way <= 0))
            def _():
                z_copy(s, way).wait_send()

        @pl.when(s != c)
        def _():
            if xr:
                x_copy(s).wait_send()
            o_copy(s, c).wait_send()

        cz_copy(s, t).wait_send()
        if xr:
            cx_copy(s, t).wait_send()
        p_copy(s).wait_send()
        for l in range(local_n):
            h_copy(s, l).wait_send()
        return carry

    lax.fori_loop(0, ctx_n, drain, 0)


def fused_path(
    tokens, routes, route_gates, up_weight, down_weight, factor_seeds,
    up_left, up_right, down_left, down_right,
):
    ctx_n, tp_n = lax.axis_size("ctx"), lax.axis_size("tp")
    n = ctx_n * tp_n
    local_n, width, half = up_weight.shape
    out_w = down_weight.shape[2]
    tok, top = routes.shape
    experts = n * local_n
    cap = 4 * tok * top // (3 * experts)
    f32, bf = jnp.float32, jnp.bfloat16
    meta_rows = -(-2 * local_n // 8) * 8
    zr = tok
    slots = tp_n * cap
    vm, anyspace = pl.BlockSpec(memory_space=pltpu.VMEM), pl.BlockSpec(memory_space=pl.ANY)
    dma = pltpu.SemaphoreType.DMA
    return pl.pallas_call(
        functools.partial(fused_kernel, (ctx_n, tp_n, local_n, cap, zr)),
        out_shape=jax.ShapeDtypeStruct((tok, out_w), bf),
        in_specs=[
            pl.BlockSpec(memory_space=pltpu.SMEM), vm, vm, anyspace, vm, vm, vm, vm,
            anyspace, anyspace,
        ],
        out_specs=vm,
        scratch_shapes=[
            pltpu.VMEM((ctx_n, tp_n, tok, width), bf),
            pltpu.VMEM((n, meta_rows, tok), f32),
            pltpu.VMEM((n, meta_rows, tok), f32),
            pltpu.VMEM((local_n, 1, width), f32),
            pltpu.VMEM((local_n, 1, half), f32),
            pltpu.VMEM((local_n, 2, 1, half), f32),
            pltpu.VMEM((local_n, 1, out_w), f32),
            pltpu.VMEM((local_n, width, half), bf),
            pltpu.VMEM((local_n, 2, out_w, half), bf),
            pltpu.VMEM((local_n, slots, width), bf),
            pltpu.VMEM((ctx_n, local_n, slots, half), bf),
            pltpu.VMEM((ctx_n, local_n, slots, half), bf),
            pltpu.VMEM((tp_n, local_n * cap, out_w), bf),
            pltpu.VMEM((2, tok, out_w), f32),
            pltpu.VMEM((ctx_n, tok, out_w), bf),
            pltpu.VMEM((ctx_n, tok, out_w), bf),
            pltpu.VMEM((ctx_n, tok, out_w), bf),
            pltpu.VMEM((ctx_n, tok, out_w), bf),
            pltpu.VMEM((tok, out_w), f32),
            dma((ctx_n, 2)), dma((ctx_n,)), dma((ctx_n,)), dma((ctx_n,)),
            dma((ctx_n,)), dma((ctx_n,)), dma((ctx_n,)), dma((ctx_n,)),
            dma((ctx_n, local_n)), dma((ctx_n, local_n)), dma((ctx_n,)), dma((ctx_n,)),
            dma((ctx_n,)), dma((ctx_n,)), dma((n,)), dma((n,)), dma((2 + 2 * local_n,)),
        ],
        compiler_params=pltpu.CompilerParams(
            collective_id=0, has_side_effects=True, vmem_limit_bytes=60 * 1024 * 1024
        ),
    )(
        factor_seeds, routes.T, route_gates.T, tokens, up_left, up_right, down_left, down_right,
        up_weight, jnp.swapaxes(down_weight, 1, 2),
    )


def on_device(*args):
    tokens, routes, up_weight, down_weight = args[0], args[1], args[3], args[4]
    experts = lax.axis_size("ctx") * lax.axis_size("tp") * up_weight.shape[0]
    cap = 4 * routes.shape[0] * routes.shape[1] // (3 * experts)
    fits = (
        lax.axis_size("exp") == 2
        and lax.axis_size("tp") == 2
        and up_weight.shape[2] % 128 == 0
        and tokens.shape[0] % 128 == 0
        and cap % 16 == 0
        and lax.axis_size("ctx") * tokens.size <= 1 << 21
        and up_weight.size + down_weight.size <= 5 << 21
    )
    return fused_path(*args) if fits else general_path(*args)


def solution(mesh):
    in_specs = (
        P(("pop", "ctx", "tp"), None),
        P(("pop", "ctx", "tp"), None),
        P(("pop", "ctx", "tp"), None),
        P(("ctx", "tp"), None, "exp"),
        P(("ctx", "tp"), None, "exp"),
        P(("pop", "ctx", "tp"), None),
        P(),
        P(None, "exp"),
        P(),
        P(None, "exp"),
    )
    out_specs = P(("pop", "ctx", "tp"), "exp")
    return jax.shard_map(
        on_device, mesh=mesh, in_specs=in_specs, out_specs=out_specs, check_vma=False
    )
```
